32 devices in a mesh: rows: 4 (over z), tm: 8 (over y, x, core).
Axes of the slice: x: 2, y: 2, z: 4, core: 2. Of those that a mesh axis runs over, the one named last changes fastest.
Arguments:
- frames_in: bfloat16 [4, 2048, 512], P('rows', 'tm'), may hold values from -6 to 6
- segment_ids: int32 [4, 2048], P('rows', 'tm'), may hold values from 0 to 3, never falling along the last dimension, each value on 1 to 1280 neighbouring positions
- cotangent: bfloat16 [4, 2048, 512], P('rows', 'tm'), may hold values from -6 to 6
- gains: bfloat16 [6, 512], replicated, may hold values from 0.099609375 to 1.8984375
- expand_one: bfloat16 [512, 2048], replicated, may hold values from -0.25 to 0.25
- shrink_one: bfloat16 [2048, 512], replicated, may hold values from -0.125 to 0.125
- query_proj: bfloat16 [512, 512], replicated, may hold values from -0.25 to 0.25
- key_proj: bfloat16 [512, 512], replicated, may hold values from -0.25 to 0.25
- value_proj: bfloat16 [512, 512], replicated, may hold values from -0.25 to 0.25
- output_proj: bfloat16 [512, 512], replicated, may hold values from -3 to 3
- conv_expand: bfloat16 [512, 1024], replicated, may hold values from -0.25 to 0.25
- conv_depth: bfloat16 [15, 512], replicated, may hold values from -1.5 to 1.5
- conv_shrink: bfloat16 [512, 512], replicated, may hold values from -0.25 to 0.25
- expand_two: bfloat16 [512, 2048], replicated, may hold values from -0.25 to 0.25
- shrink_two: bfloat16 [2048, 512], replicated, may hold values from -0.125 to 0.125
Outputs:
- layer_out: bfloat16 [4, 2048, 512], P('rows', 'tm')
- input_grad: bfloat16 [4, 2048, 512], P('rows', 'tm')
- gains_grad: float32 [6, 512], replicated
- expand_one_grad: float32 [512, 2048], P('tm')
- shrink_one_grad: float32 [2048, 512], P('tm')
- query_proj_grad: float32 [512, 512], P('tm')
- key_proj_grad: float32 [512, 512], P('tm')
- value_proj_grad: float32 [512, 512], P('tm')
- output_proj_grad: float32 [512, 512], P('tm')
- conv_expand_grad: float32 [512, 1024], P('tm')
- conv_depth_grad: float32 [15, 512], replicated
- conv_shrink_grad: float32 [512, 512], P('tm')
- expand_two_grad: float32 [512, 2048], P('tm')
- shrink_two_grad: float32 [2048, 512], P('tm')
The draws below stay inside these ranges and needn't reach their ends.
Inputs may be any that keep to these rules, and one draw needn't show every extreme that they name: `segment_ids`: along each row the ids never fall; an utterance spans 1 to 1280 frames and one spans exactly 1280.
All inputs are finite; a program needn't handle non-finite values.
Results may differ from the reference program's by a relative error of at most 0.019.
Values may be sent and summed in bfloat16 or wider, within the bound.
No kernel may reach another device: no remote copies, remote signals or barrier semaphores. Data moves between devices by JAX's collectives and lax.ppermute only.
A program may use at most 256 MiB of HBM per device.

```python
import math
import jax
import jax.numpy as jnp
import numpy as np
from jax import lax

D = 512
HEADS = 8
HEAD_DIM = 64
FF = 2048
KW = 15
SEG_COUNT = 4
F_DEV = 256
ROWS = 4
FRAMES = 2048
SEG_MOST = 1280
N_TM = 8


def block_scale(key, shape, cuts, low, top_value):
    def one(dim, parts):
        heights = jax.random.uniform(jax.random.fold_in(jax.random.fold_in(key, 6), dim), (parts,), jnp.float32, low / len(cuts), top_value / len(cuts))
        return jnp.repeat(jnp.exp(heights), shape[dim] // parts).reshape((-1,) + (1,) * (len(shape) - dim - 1))

    factor_of = one(*cuts[0])
    for cut in cuts[1:]:
        factor_of = factor_of * one(*cut)
    return factor_of


def length_profile(number_of, total, reach, lean):
    portions = [(1 << 20) // math.isqrt(standing ** lean) + 1 for standing in range(2, number_of + 1)]
    spare, given = total - reach - (number_of - 1), [1] * (number_of - 1)
    while spare > 0:
        candidates = [i for i in range(number_of - 1) if given[i] < reach]
        mass, budget = sum([portions[i] for i in candidates]), spare
        for i in candidates:
            extra = min(reach - given[i], max(1, budget * portions[i] // mass), spare)
            given[i] = given[i] + extra
            spare = spare - extra
    return np.array([reach] + given)


def uneven(rng, number_of, total, bound, slope):
    if number_of == 2:
        one = jax.random.randint(rng, (), max(1, total - bound), min(bound, total - 1) + 1)
        return jnp.stack([one, total - one])
    tallies = jnp.asarray(length_profile(number_of, total, bound, slope), jnp.int32)
    pairs = (number_of - 1) // 2
    giver, receiver = tallies[1:1 + 2 * pairs:2], tallies[2:2 + 2 * pairs:2]
    margin = jnp.minimum(giver - 1, bound - receiver)
    moved = jax.random.randint(jax.random.fold_in(rng, 1), (pairs,), 0, 1 << 20) % (margin + 1)
    tallies = tallies.at[1:1 + 2 * pairs:2].set(giver - moved).at[2:2 + 2 * pairs:2].set(receiver + moved)
    return tallies[jax.random.permutation(jax.random.fold_in(rng, 2), number_of)]


def scatter_about(stream_key, shape, width, most, pieces=(), held_as=jnp.bfloat16):
    result = width * jax.random.normal(stream_key, shape, jnp.float32)
    if pieces:
        result = result * block_scale(stream_key, shape, pieces, -0.22, 0.18)
    return jnp.clip(result, -most, most).astype(held_as)


def setup_inputs(seed: int = 0) -> dict:
    seeds = jax.random.split(jax.random.key(seed), 16)
    return {
        "frames_in": scatter_about(seeds[0], (ROWS, FRAMES, D), 1.0, 6.0, ((0, 4), (1, 8))),
        "segment_ids": jax.vmap(lambda own: jnp.searchsorted(jnp.cumsum(uneven(own, SEG_COUNT, FRAMES, SEG_MOST, 0)), jnp.arange(FRAMES), side="right"))(jax.random.split(seeds[1], ROWS)).reshape((ROWS, FRAMES)).astype(jnp.int32),
        "cotangent": scatter_about(seeds[2], (ROWS, FRAMES, D), 1.0, 6.0, ((0, 4), (1, 8))),
        "gains": jnp.clip(1.0 + 0.18 * jax.random.normal(seeds[3], (6, D), jnp.float32), 0.099609375, 1.8984375).astype(jnp.bfloat16),
        "expand_one": scatter_about(seeds[4], (D, FF), D ** -0.5, 0.25),
        "shrink_one": scatter_about(seeds[5], (FF, D), FF ** -0.5, 0.125),
        "query_proj": scatter_about(seeds[6], (D, D), D ** -0.5, 0.25),
        "key_proj": scatter_about(seeds[7], (D, D), D ** -0.5, 0.25),
        "value_proj": scatter_about(seeds[8], (D, D), D ** -0.5, 0.25),
        "output_proj": scatter_about(seeds[9], (D, D), (max(1, 10000 // (F_DEV * N_TM))) ** -0.5, 3.0),
        "conv_expand": scatter_about(seeds[10], (D, 2 * D), D ** -0.5, 0.25),
        "conv_depth": scatter_about(seeds[11], (KW, D), KW ** -0.5, 1.5),
        "conv_shrink": scatter_about(seeds[12], (D, D), D ** -0.5, 0.25),
        "expand_two": scatter_about(seeds[13], (D, FF), D ** -0.5, 0.25),
        "shrink_two": scatter_about(seeds[14], (FF, D), FF ** -0.5, 0.125),
    }


@jax.custom_vjp
def low(v):
    return lax.optimization_barrier(v.astype(jnp.bfloat16)).astype(jnp.float32)

@jax.custom_vjp
def low_back(v):
    return v

def low_keep(v):
    return (low(v), None)

def low_pass(kept, grad):
    return (grad,)

def back_keep(v):
    return (v, None)

def back_low(kept, grad):
    return (low(grad),)
low.defvjp(low_keep, low_pass)
low_back.defvjp(back_keep, back_low)
highest = lax.Precision.HIGHEST

def matmul(left_side, right_side):
    return jnp.dot(left_side, right_side, precision=highest, preferred_element_type=jnp.float32)

def normalize(values):
    centered = values - lax.optimization_barrier(jnp.mean(values, axis=-1, keepdims=True))
    variance = lax.optimization_barrier(jnp.mean(centered * centered, axis=-1, keepdims=True))
    return centered * lax.rsqrt(variance + 1e-05)

def rotary_tables(positions):
    half_dim = HEAD_DIM // 2
    frequency = jnp.power(10000.0, -jnp.arange(half_dim, dtype=jnp.float32) / half_dim)
    angles = positions[:, None] * frequency[None, :]
    return (jnp.cos(angles)[:, None, :], jnp.sin(angles)[:, None, :])

def rotate(values, cosine_table, sine_table):
    half_dim = values.shape[-1] // 2
    first_half = values[..., :half_dim]
    second_half = values[..., half_dim:]
    return jnp.concatenate([first_half * cosine_table - second_half * sine_table, first_half * sine_table + second_half * cosine_table], axis=-1)

def feed_forward(values, gain_row, weight_in, weight_out):
    hidden = low(normalize(values) * gain_row)
    activation = low_back(matmul(hidden, weight_in))
    activation = low(activation * jax.nn.sigmoid(activation))
    return values + 0.5 * low_back(matmul(activation, weight_out))

def attention(values, gain_row, query_proj, key_proj, value_proj, output_proj, segment_row):
    frames = values.shape[0]
    hidden = low(normalize(values) * gain_row)
    shaped = (frames, HEADS, HEAD_DIM)
    queries = low_back(matmul(hidden, query_proj)).reshape(shaped)
    keys = low_back(matmul(hidden, key_proj)).reshape(shaped)
    value_heads = low(low_back(matmul(hidden, value_proj))).reshape(shaped)
    positions = jnp.arange(frames, dtype=jnp.int32).astype(jnp.float32)
    cosine_table, sine_table = rotary_tables(positions)
    queries = low(rotate(queries, cosine_table, sine_table) * 0.125)
    keys = low(rotate(keys, cosine_table, sine_table))
    block_rows = min(512, frames)
    block_count = frames // block_rows
    columns = jnp.arange(frames, dtype=jnp.int32)

    def one_block(element):
        query_block, start_row = element
        scores = jnp.einsum('qhd,khd->hqk', query_block, keys, precision=highest, preferred_element_type=jnp.float32)
        scores = low_back(scores)
        row_index = start_row + jnp.arange(block_rows, dtype=jnp.int32)
        row_segs = lax.dynamic_slice_in_dim(segment_row, start_row, block_rows)
        visible = (columns[None, :] <= row_index[:, None]) & (segment_row[None, :] == row_segs[:, None])
        masked = jnp.where(visible[None], scores, -1e+30)
        shifted = jnp.exp(masked - lax.optimization_barrier(jnp.max(masked, axis=-1, keepdims=True)))
        weights = low(shifted / lax.optimization_barrier(jnp.sum(shifted, axis=-1, keepdims=True)))
        return low_back(jnp.einsum('hqk,khd->qhd', weights, value_heads, precision=highest, preferred_element_type=jnp.float32))
    starts = jnp.arange(block_count, dtype=jnp.int32) * block_rows
    attended = lax.map(jax.checkpoint(one_block), (queries.reshape(block_count, block_rows, HEADS, HEAD_DIM), starts))
    attended = low(attended.reshape(frames, HEADS * HEAD_DIM))
    return values + low_back(matmul(attended, output_proj))

def convolve(values, gain_in, gain_mid, conv_expand, conv_depth, conv_shrink, segment_row):
    frames = values.shape[0]
    hidden = low(normalize(values) * gain_in)
    pointwise = low_back(matmul(hidden, conv_expand))
    gated = low(pointwise[:, :D] * jax.nn.sigmoid(pointwise[:, D:]))
    padded = jnp.concatenate([jnp.zeros((KW - 1, D), jnp.float32), gated], axis=0)
    padded_seg = jnp.concatenate([jnp.full((KW - 1,), -1, jnp.int32), segment_row])
    mixed_taps = jnp.zeros((frames, D), jnp.float32)
    for tap_index in range(KW):
        offset = KW - 1 - tap_index
        same_utterance = (padded_seg[offset:offset + frames] == segment_row)[:, None]
        mixed_taps = mixed_taps + jnp.where(same_utterance, conv_depth[tap_index] * padded[offset:offset + frames], 0.0)
    inner_gate = normalize(mixed_taps) * gain_mid
    inner_gate = low(inner_gate * jax.nn.sigmoid(inner_gate))
    return values + low_back(matmul(inner_gate, conv_shrink))

def layer(values, gain_rows, weights, segment_row):
    expand_one, shrink_one, query_proj, key_proj, value_proj, output_proj, conv_expand, conv_depth, conv_shrink, expand_two, shrink_two = weights
    hidden = feed_forward(values, gain_rows[0], expand_one, shrink_one)
    hidden = attention(hidden, gain_rows[1], query_proj, key_proj, value_proj, output_proj, segment_row)
    hidden = convolve(hidden, gain_rows[2], gain_rows[3], conv_expand, conv_depth, conv_shrink, segment_row)
    hidden = feed_forward(hidden, gain_rows[4], expand_two, shrink_two)
    return normalize(hidden) * gain_rows[5]

def reference(frames_in, segment_ids, cotangent, gains, expand_one, shrink_one, query_proj, key_proj, value_proj, output_proj, conv_expand, conv_depth, conv_shrink, expand_two, shrink_two):
    gain_rows = gains.astype(jnp.float32)
    weights = tuple((item.astype(jnp.float32) for item in (expand_one, shrink_one, query_proj, key_proj, value_proj, output_proj, conv_expand, conv_depth, conv_shrink, expand_two, shrink_two)))

    def per_row(carried, row_data):
        row_frames, row_segs, row_cot = row_data

        def forward(values, gain_values, weight_values):
            return layer(values, gain_values, weight_values, row_segs)
        output, pullback = jax.vjp(forward, row_frames.astype(jnp.float32), gain_rows, weights)
        grad_frames, grad_gains, grad_weights = pullback(row_cot.astype(jnp.float32))
        carried = (carried[0] + grad_gains, tuple((left_side + right_side for left_side, right_side in zip(carried[1], grad_weights))))
        return (carried, (output.astype(jnp.bfloat16), grad_frames.astype(jnp.bfloat16)))
    initial = (jnp.zeros_like(gain_rows), tuple((jnp.zeros_like(item) for item in weights)))
    (grad_gains, grad_weights), (outputs, grad_inputs) = lax.scan(per_row, initial, (frames_in, segment_ids, cotangent))
    return (outputs, grad_inputs, grad_gains, grad_weights[0], grad_weights[1], grad_weights[2], grad_weights[3], grad_weights[4], grad_weights[5], grad_weights[6], grad_weights[7], grad_weights[8], grad_weights[9], grad_weights[10])
```

```python
import jax
import jax.numpy as jnp
from jax import lax
from jax.sharding import PartitionSpec as P

HEADS = 8
HEAD_DIM = 64


def passed_along(value, axis, steps):
    count = lax.axis_size(axis)
    first, last = (max(0, -steps), min(count, count - steps))
    return lax.ppermute(value, axis, [(source, source + steps) for source in range(first, last)])


def swapped(value, axis, bit):
    count = lax.axis_size(axis)
    return lax.ppermute(value, axis, [(i, i ^ bit) for i in range(count)])


def halve(value, axis, order):
    index = lax.axis_index(axis)
    left = list(range(value.shape[0].bit_length() - 1))[::-1]
    value = value.reshape((2,) * len(left) + value.shape[1:])
    for bit in order:
        place = left.index(bit.bit_length() - 1)
        mine = (index // bit) % 2
        theirs = lax.dynamic_index_in_dim(value, 1 - mine, place, keepdims=False)
        kept = lax.dynamic_index_in_dim(value, mine, place, keepdims=False)
        value = (
            kept.astype(jnp.float32) + swapped(theirs, axis, bit).astype(jnp.float32)
        ).astype(jnp.bfloat16)
        left.pop(place)
    return value


def sum_rows(value):
    index = lax.axis_index("rows")
    count = lax.axis_size("rows")
    rows, width = value.shape
    own = halve(value.reshape(count, rows // count, width), "rows", (1, 2))
    other = swapped(own, "rows", 2)
    high = (index // 2) % 2
    low = index % 2
    pair = jnp.where(high == 0, jnp.stack([own, other]), jnp.stack([other, own]))
    others = swapped(pair, "rows", 1)
    both = jnp.where(low == 0, jnp.stack([pair, others], 1), jnp.stack([others, pair], 1))
    return both.reshape(rows, width)


def matmul(left_side, right_side):
    return jnp.dot(left_side, right_side, preferred_element_type=jnp.float32)


def outer_sum(left_side, right_side):
    return jnp.einsum("fa,fb->ab", left_side, right_side, preferred_element_type=jnp.float32)


def back_matmul(gradient, weight):
    return jnp.einsum("fb,ab->fa", gradient, weight, preferred_element_type=jnp.float32)


def normalize(values):
    centered = values - jnp.mean(values, axis=-1, keepdims=True)
    inverse = lax.rsqrt(jnp.mean(centered * centered, axis=-1, keepdims=True) + 1e-05)
    return (centered * inverse, inverse)


def norm_back(gradient, normed, inverse):
    return inverse * (
        gradient
        - jnp.mean(gradient, axis=-1, keepdims=True)
        - normed * jnp.mean(gradient * normed, axis=-1, keepdims=True)
    )


def swish_grad(values):
    squashed = jax.nn.sigmoid(values)
    return squashed * (1.0 + values * (1.0 - squashed))


def rotary_tables(positions):
    half_dim = HEAD_DIM // 2
    frequency = jnp.power(10000.0, -jnp.arange(half_dim, dtype=jnp.float32) / half_dim)
    angles = positions[:, None] * frequency[None, :]
    return (jnp.cos(angles)[:, None, :], jnp.sin(angles)[:, None, :])


def rotate(values, cosine_table, sine_table):
    half_dim = values.shape[-1] // 2
    first_half = values[..., :half_dim]
    second_half = values[..., half_dim:]
    return jnp.concatenate(
        [
            first_half * cosine_table - second_half * sine_table,
            first_half * sine_table + second_half * cosine_table,
        ],
        axis=-1,
    )


def unrotate(values, cosine_table, sine_table):
    half_dim = values.shape[-1] // 2
    first_half = values[..., :half_dim]
    second_half = values[..., half_dim:]
    return jnp.concatenate(
        [
            first_half * cosine_table + second_half * sine_table,
            second_half * cosine_table - first_half * sine_table,
        ],
        axis=-1,
    )


def ffn_forward(inputs, gain_row, weight_in, weight_out):
    normed, inverse = normalize(inputs)
    hidden = (normed * gain_row).astype(jnp.bfloat16)
    activation = matmul(hidden, weight_in)
    squashed = (activation * jax.nn.sigmoid(activation)).astype(jnp.bfloat16)
    return (
        inputs + 0.5 * matmul(squashed, weight_out),
        (normed, inverse, hidden, activation, squashed),
    )


def ffn_backward(gradient, gain_row, weight_in, weight_out, stored):
    normed, inverse, hidden, activation, squashed = stored
    half_grad = (0.5 * gradient).astype(jnp.bfloat16)
    grad_out = outer_sum(squashed, half_grad)
    grad_act = (back_matmul(half_grad, weight_out) * swish_grad(activation)).astype(jnp.bfloat16)
    grad_in = outer_sum(hidden, grad_act)
    grad_hidden = back_matmul(grad_act, weight_in)
    grad_gain = jnp.sum(grad_hidden * normed, axis=0)
    return (
        gradient + norm_back(grad_hidden * gain_row, normed, inverse),
        grad_gain,
        grad_in,
        grad_out,
    )


def visibility(query_pos, query_seg, key_pos, key_seg):
    return ((key_pos[None, :] <= query_pos[:, None]) & (key_seg[None, :] == query_seg[:, None]))[
        None
    ]


def attend(running, queries, key_block, value_block, query_pos, query_seg, key_pos, key_seg):
    running_max, running_sum, accumulated = running
    scores = jnp.einsum("qhd,khd->hqk", queries, key_block, preferred_element_type=jnp.float32)
    visible = visibility(query_pos, query_seg, key_pos, key_seg)
    new_max = jnp.maximum(running_max, jnp.max(jnp.where(visible, scores, -1e30), axis=-1))
    factor = jnp.exp(running_max - new_max)
    weights = jnp.where(visible, jnp.exp(scores - new_max[:, :, None]), 0.0)
    running_sum = running_sum * factor + jnp.sum(weights, axis=-1)
    update = jnp.einsum(
        "hqk,khd->qhd",
        weights.astype(jnp.bfloat16),
        value_block,
        preferred_element_type=jnp.float32,
    )
    accumulated = accumulated * jnp.transpose(factor)[:, :, None] + update
    return (new_max, running_sum, accumulated)


def score_terms(
    queries,
    grad_heads,
    log_total,
    row_delta,
    query_pos,
    query_seg,
    key_block,
    value_block,
    key_pos,
    key_seg,
):
    scores = jnp.einsum("qhd,khd->hqk", queries, key_block, preferred_element_type=jnp.float32)
    visible = visibility(query_pos, query_seg, key_pos, key_seg)
    weights = jnp.where(visible, jnp.exp(scores - log_total[:, :, None]), 0.0)
    grad_weights = jnp.einsum(
        "qhd,khd->hqk", grad_heads, value_block, preferred_element_type=jnp.float32
    )
    grad_scores = (weights * (grad_weights - row_delta[:, :, None])).astype(jnp.bfloat16)
    return (weights.astype(jnp.bfloat16), grad_scores)


def shards(
    frames_in,
    segment_ids,
    cotangent,
    gains,
    expand_one,
    shrink_one,
    query_proj,
    key_proj,
    value_proj,
    output_proj,
    conv_expand,
    conv_depth,
    conv_shrink,
    expand_two,
    shrink_two,
):
    frames_dev = frames_in.shape[1]
    model_width = frames_in.shape[2]
    kernel = conv_depth.shape[0]
    shaped = (frames_dev, HEADS, HEAD_DIM)
    inputs = frames_in[0].astype(jnp.float32)
    gain_rows = gains.astype(jnp.float32)
    depth = conv_depth.astype(jnp.float32)
    own_seg = segment_ids[0]
    full_seg = lax.all_gather(own_seg, "tm", axis=0, tiled=True)
    row_offset = lax.axis_index("tm") * frames_dev
    query_pos = row_offset + jnp.arange(frames_dev, dtype=jnp.int32)
    cosine_table, sine_table = rotary_tables(query_pos.astype(jnp.float32))
    first_out, first_kept = ffn_forward(inputs, gain_rows[0], expand_one, shrink_one)
    normed_attn, inverse_attn = normalize(first_out)
    hidden_attn = (normed_attn * gain_rows[1]).astype(jnp.bfloat16)
    queries = (
        rotate(matmul(hidden_attn, query_proj).reshape(shaped), cosine_table, sine_table) * 0.125
    ).astype(jnp.bfloat16)
    keys_rot = rotate(
        matmul(hidden_attn, key_proj).reshape(shaped), cosine_table, sine_table
    ).astype(jnp.bfloat16)
    values_flat = matmul(hidden_attn, value_proj).astype(jnp.bfloat16)
    keys_flat = keys_rot.reshape(frames_dev, model_width)
    initial = (
        jnp.full((HEADS, frames_dev), -1e30, jnp.float32),
        jnp.zeros((HEADS, frames_dev), jnp.float32),
        jnp.zeros(shaped, jnp.float32),
    )
    carried = initial
    key_piece = lax.all_gather(keys_flat, "tm", axis=0, tiled=True)
    value_piece = lax.all_gather(values_flat, "tm", axis=0, tiled=True)
    piece_rows = key_piece.shape[0]
    fold_block_rows = 1024
    block_count = piece_rows // fold_block_rows
    key_blocks = key_piece.reshape(block_count, fold_block_rows, HEADS, HEAD_DIM)
    value_blocks = value_piece.reshape(block_count, fold_block_rows, HEADS, HEAD_DIM)
    offsets = jnp.arange(block_count, dtype=jnp.int32) * fold_block_rows

    def step(running, element):
        key_block, value_block, offset = element
        key_pos = offset + jnp.arange(fold_block_rows, dtype=jnp.int32)
        key_seg = lax.dynamic_slice_in_dim(full_seg, offset, fold_block_rows)
        return (
            attend(running, queries, key_block, value_block, query_pos, own_seg, key_pos, key_seg),
            None,
        )

    carried, _ = lax.scan(step, carried, (key_blocks, value_blocks, offsets))
    running_max, running_sum, accumulated = carried
    log_total = running_max + jnp.log(running_sum)
    attended = accumulated / jnp.transpose(running_sum)[:, :, None]
    attended_low = attended.reshape(frames_dev, model_width).astype(jnp.bfloat16)
    second_out = first_out + matmul(attended_low, output_proj)
    normed_conv, inverse_conv = normalize(second_out)
    hidden_conv = (normed_conv * gain_rows[2]).astype(jnp.bfloat16)
    pointwise = matmul(hidden_conv, conv_expand)
    linear_half = pointwise[:, :model_width]
    gate_sig = jax.nn.sigmoid(pointwise[:, model_width:])
    gated_low = (linear_half * gate_sig).astype(jnp.bfloat16)
    halo_rows = passed_along(gated_low[frames_dev - kernel + 1 :], "tm", 1)
    extended = jnp.concatenate([halo_rows, gated_low], axis=0).astype(jnp.float32)
    padded_seg = jnp.concatenate([jnp.full((kernel - 1,), -1, jnp.int32), full_seg])
    extended_seg = lax.dynamic_slice_in_dim(padded_seg, row_offset, frames_dev + kernel - 1)
    tap_masks = []
    mixed_taps = jnp.zeros((frames_dev, model_width), jnp.float32)
    for tap_index in range(kernel):
        offset = kernel - 1 - tap_index
        same_utterance = (extended_seg[offset : offset + frames_dev] == own_seg).astype(
            jnp.float32
        )[:, None]
        tap_masks.append(same_utterance)
        mixed_taps = (
            mixed_taps + same_utterance * depth[tap_index] * extended[offset : offset + frames_dev]
        )
    normed_mid, inverse_mid = normalize(mixed_taps)
    inner_gate = normed_mid * gain_rows[3]
    inner_low = (inner_gate * jax.nn.sigmoid(inner_gate)).astype(jnp.bfloat16)
    third_out = second_out + matmul(inner_low, conv_shrink)
    fourth_out, fourth_kept = ffn_forward(third_out, gain_rows[4], expand_two, shrink_two)
    normed_last, inverse_last = normalize(fourth_out)
    layer_out = (normed_last * gain_rows[5]).astype(jnp.bfloat16)
    gradient = cotangent[0].astype(jnp.float32)
    grad_gain_last = jnp.sum(gradient * normed_last, axis=0)
    gradient = norm_back(gradient * gain_rows[5], normed_last, inverse_last)
    gradient, grad_gain_four, grad_expand_two, grad_shrink_two = ffn_backward(
        gradient, gain_rows[4], expand_two, shrink_two, fourth_kept
    )
    grad_conv_low = gradient.astype(jnp.bfloat16)
    grad_conv_shrink = outer_sum(inner_low, grad_conv_low)
    grad_inner = back_matmul(grad_conv_low, conv_shrink) * swish_grad(inner_gate)
    grad_gain_mid = jnp.sum(grad_inner * normed_mid, axis=0)
    grad_mixed = norm_back(grad_inner * gain_rows[3], normed_mid, inverse_mid)
    grad_extended = jnp.zeros((frames_dev + kernel - 1, model_width), jnp.float32)
    depth_rows = []
    for tap_index in range(kernel):
        offset = kernel - 1 - tap_index
        masked_grad = grad_mixed * tap_masks[tap_index]
        depth_rows.append(jnp.sum(masked_grad * extended[offset : offset + frames_dev], axis=0))
        grad_extended = grad_extended.at[offset : offset + frames_dev].add(
            masked_grad * depth[tap_index]
        )
    grad_depth = jnp.stack(depth_rows)
    returned = passed_along(grad_extended[: kernel - 1], "tm", -1)
    grad_gated = grad_extended[kernel - 1 :] + jnp.concatenate(
        [jnp.zeros((frames_dev - kernel + 1, model_width), jnp.float32), returned], axis=0
    )
    grad_pointwise = jnp.concatenate(
        [grad_gated * gate_sig, grad_gated * linear_half * gate_sig * (1.0 - gate_sig)], axis=1
    ).astype(jnp.bfloat16)
    grad_conv_expand = outer_sum(hidden_conv, grad_pointwise)
    grad_hidden = back_matmul(grad_pointwise, conv_expand)
    grad_gain_conv = jnp.sum(grad_hidden * normed_conv, axis=0)
    gradient = gradient + norm_back(grad_hidden * gain_rows[2], normed_conv, inverse_conv)
    grad_attn_low = gradient.astype(jnp.bfloat16)
    grad_output_proj = outer_sum(attended_low, grad_attn_low)
    grad_heads = back_matmul(grad_attn_low, output_proj).reshape(shaped).astype(jnp.bfloat16)
    row_delta = jnp.einsum("qhd,qhd->hq", grad_heads.astype(jnp.float32), attended)
    all_keys, all_values = (
        lax.all_gather(keys_flat, "tm", axis=0, tiled=True),
        lax.all_gather(values_flat, "tm", axis=0, tiled=True),
    )
    frames_all = all_keys.shape[0]
    block_rows = min(1024, frames_all)
    block_offsets = jnp.arange(frames_all // block_rows, dtype=jnp.int32) * block_rows

    def joint_step(grad_queries, offset):
        key_block = lax.dynamic_slice_in_dim(all_keys, offset, block_rows).reshape(
            block_rows, HEADS, HEAD_DIM
        )
        value_block = lax.dynamic_slice_in_dim(all_values, offset, block_rows).reshape(
            block_rows, HEADS, HEAD_DIM
        )
        key_pos = offset + jnp.arange(block_rows, dtype=jnp.int32)
        key_seg = lax.dynamic_slice_in_dim(full_seg, offset, block_rows)
        weights_low, grad_scores = score_terms(
            queries,
            grad_heads,
            log_total,
            row_delta,
            query_pos,
            own_seg,
            key_block,
            value_block,
            key_pos,
            key_seg,
        )
        grad_queries = grad_queries + jnp.einsum(
            "hqk,khd->qhd", grad_scores, key_block, preferred_element_type=jnp.float32
        )
        grad_keys = jnp.einsum(
            "hqk,qhd->khd", grad_scores, queries, preferred_element_type=jnp.float32
        )
        grad_vals = jnp.einsum(
            "hqk,qhd->khd", weights_low, grad_heads, preferred_element_type=jnp.float32
        )
        term_block = jnp.concatenate(
            [
                grad_keys.reshape(block_rows, model_width),
                grad_vals.reshape(block_rows, model_width),
            ],
            axis=1,
        )
        return (grad_queries, term_block)

    grad_rot_q, term_blocks = lax.scan(joint_step, jnp.zeros(shaped, jnp.float32), block_offsets)
    key_sums = lax.psum_scatter(
        term_blocks.reshape(frames_all, 2 * model_width), "tm", scatter_dimension=0, tiled=True
    )
    grad_rot_k = key_sums[:, :model_width].reshape(shaped)
    grad_values = key_sums[:, model_width:]
    grad_query_low = (
        (unrotate(grad_rot_q, cosine_table, sine_table) * 0.125)
        .reshape(frames_dev, model_width)
        .astype(jnp.bfloat16)
    )
    grad_key_low = (
        unrotate(grad_rot_k, cosine_table, sine_table)
        .reshape(frames_dev, model_width)
        .astype(jnp.bfloat16)
    )
    grad_value_low = grad_values.astype(jnp.bfloat16)
    grad_query_proj = outer_sum(hidden_attn, grad_query_low)
    grad_key_proj = outer_sum(hidden_attn, grad_key_low)
    grad_value_proj = outer_sum(hidden_attn, grad_value_low)
    grad_hidden = (
        back_matmul(grad_query_low, query_proj)
        + back_matmul(grad_key_low, key_proj)
        + back_matmul(grad_value_low, value_proj)
    )
    grad_gain_attn = jnp.sum(grad_hidden * normed_attn, axis=0)
    gradient = gradient + norm_back(grad_hidden * gain_rows[1], normed_attn, inverse_attn)
    gradient, grad_gain_one, grad_expand_one, grad_shrink_one = ffn_backward(
        gradient, gain_rows[0], expand_one, shrink_one, first_kept
    )
    count = lax.axis_size("tm")
    pieces = [
        grad_expand_one, grad_shrink_one, grad_query_proj, grad_key_proj, grad_value_proj,
        grad_output_proj, grad_conv_expand, grad_conv_shrink, grad_expand_two, grad_shrink_two,
    ]
    stacked = jnp.concatenate(
        [item.astype(jnp.bfloat16).reshape(count, -1, 512) for item in pieces], axis=1
    )
    rows_total = stacked.shape[1]
    half = rows_total // 2
    bits = [1 << i for i in range(count.bit_length() - 1)]
    orders = [bits, bits[:1] + bits[:0:-1]]
    parts = [halve(stacked[:, :half], "tm", orders[0]), halve(stacked[:, half:], "tm", orders[1])]
    summed = jnp.concatenate([sum_rows(part) for part in parts], axis=0).astype(jnp.float32)
    matrices = []
    start = 0
    for item in pieces:
        length = item.size // count // 512
        matrices.append(
            summed[start : start + length].reshape((item.shape[0] // count, item.shape[1]))
        )
        start += length
    gain_stack = jnp.concatenate(
        [
            jnp.stack(
                [
                    grad_gain_one,
                    grad_gain_attn,
                    grad_gain_conv,
                    grad_gain_mid,
                    grad_gain_four,
                    grad_gain_last,
                ]
            ),
            grad_depth,
        ]
    )
    for bit in bits:
        gain_stack = gain_stack + swapped(gain_stack, "tm", bit)
    for bit in (1, 2):
        gain_stack = gain_stack + swapped(gain_stack, "rows", bit)
    small_sums = (gain_stack[:6], gain_stack[6:])
    return (
        layer_out[None],
        gradient.astype(jnp.bfloat16)[None],
        small_sums[0],
        matrices[0],
        matrices[1],
        matrices[2],
        matrices[3],
        matrices[4],
        matrices[5],
        matrices[6],
        small_sums[1],
        matrices[7],
        matrices[8],
        matrices[9],
    )


def solution(mesh):
    return jax.shard_map(
        shards,
        mesh=mesh,
        in_specs=(
            P("rows", "tm", None),
            P("rows", "tm"),
            P("rows", "tm", None),
            P(),
            P(),
            P(),
            P(),
            P(),
            P(),
            P(),
            P(),
            P(),
            P(),
            P(),
            P(),
        ),
        out_specs=(
            P("rows", "tm", None),
            P("rows", "tm", None),
            P(),
            P("tm", None),
            P("tm", None),
            P("tm", None),
            P("tm", None),
            P("tm", None),
            P("tm", None),
            P("tm", None),
            P(),
            P("tm", None),
            P("tm", None),
            P("tm", None),
        ),
        check_vma=False,
    )
```

```python
import functools

import jax
import jax.numpy as jnp
import numpy as np
from jax import lax
from jax.experimental import pallas as pl
from jax.experimental.pallas import tpu as pltpu
from jax.sharding import PartitionSpec as P

HEADS = 8
HEAD_DIM = 64
EDGE = 16
TILE = 256
F32 = jnp.float32
BF16 = jnp.bfloat16
SMEM = pl.BlockSpec(memory_space=pltpu.SMEM)
ANY = pl.BlockSpec(memory_space=pl.ANY)
VMEM = pl.BlockSpec(memory_space=pltpu.VMEM)
ORDER = (0, 2, 4, 6, 1, 3, 5, 7)


def swapped(value, axis, bit):
    count = lax.axis_size(axis)
    return lax.ppermute(value, axis, [(i, i ^ bit) for i in range(count)])


def passed_along(value, axis, steps):
    count = lax.axis_size(axis)
    first, last = (max(0, -steps), min(count, count - steps))
    return lax.ppermute(value, axis, [(source, source + steps) for source in range(first, last)])


def all_swapped(packets):
    return [packets[0]] + [swapped(packets[i], "tm", i) for i in range(1, HEADS)]


def halve(value, axis, order):
    index = lax.axis_index(axis)
    left = list(range(value.shape[0].bit_length() - 1))[::-1]
    value = value.reshape((2,) * len(left) + value.shape[1:])
    for bit in order:
        place = left.index(bit.bit_length() - 1)
        mine = (index // bit) % 2
        theirs = lax.dynamic_index_in_dim(value, 1 - mine, place, keepdims=False)
        kept = lax.dynamic_index_in_dim(value, mine, place, keepdims=False)
        value = added(kept, swapped(theirs, axis, bit))
        left.pop(place)
    return value


def added(*values):
    total = values[0].astype(F32)
    for value in values[1:]:
        total = total + value.astype(F32)
    return total.astype(BF16)


def sum_general(stacked):
    count = lax.axis_size("tm")
    half = stacked.shape[1] // 2
    bits = [1 << i for i in range(count.bit_length() - 1)]
    orders = [bits, bits[:1] + bits[:0:-1]]
    parts = [halve(stacked[:, :half], "tm", orders[0]), halve(stacked[:, half:], "tm", orders[1])]
    return row_pieces(jnp.concatenate(parts, axis=0))


def sum_relative(kept, sent):
    half = kept.shape[1] // 2
    back = swapped(sent, "tm", 1)
    outcome = []
    for part, (first, second) in enumerate(((2, 4), (4, 2))):
        span = slice(part * half, (part + 1) * half)
        give, keep = ((1, 3), (0, 2)) if first == 2 else ((2, 3), (0, 1))
        gives = [added(kept[i, span], back[i, span]) for i in give]
        keeps = [added(kept[i, span], back[i, span]) for i in keep]
        came = swapped(jnp.stack(gives), "tm", first)
        onward = swapped(added(keeps[1], came[1]), "tm", second)
        outcome.append((keeps[0], came[0], onward))
    return row_pieces(
        jnp.concatenate([added(*items) for items in outcome], axis=0)
    )


def row_pieces(value):
    index = lax.axis_index("rows")
    count = lax.axis_size("rows")
    rows, width = value.shape
    pieces = value.reshape(count, rows // count, width)
    own = lax.dynamic_index_in_dim(pieces, index, 0, keepdims=False)
    came = [
        swapped(lax.dynamic_index_in_dim(pieces, index ^ j, 0, keepdims=False), "rows", j)
        for j in range(1, count)
    ]
    total = added(own, *came)
    return [total] + [swapped(total, "rows", j) for j in range(1, count)]


def mm(left, right):
    return jnp.dot(left, right, preferred_element_type=F32)


def mm_nt(left, right):
    return lax.dot_general(left, right, (((1,), (1,)), ((), ())), preferred_element_type=F32)


def norm(values):
    centered = values - jnp.mean(values, axis=-1, keepdims=True)
    inverse = lax.rsqrt(jnp.mean(centered * centered, axis=-1, keepdims=True) + 1e-05)
    return centered * inverse, inverse


def norm_back(gradient, normed, inverse):
    return inverse * (
        gradient
        - jnp.mean(gradient, axis=-1, keepdims=True)
        - normed * jnp.mean(gradient * normed, axis=-1, keepdims=True)
    )


def swish_grad(values):
    squashed = jax.nn.sigmoid(values)
    return squashed * (1.0 + values * (1.0 - squashed))


def low_lanes(rows):
    return lax.broadcasted_iota(jnp.int32, (rows, 128), 1) < HEAD_DIM


def joined(left, right, rows):
    return jnp.where(low_lanes(rows), left, pltpu.roll(right, HEAD_DIM, 1))


def angles(base_ref, table_ref, index):
    base = base_ref[index]
    cosine, sine = base[0:1, :], base[1:2, :]
    return (
        cosine * table_ref[0] - sine * table_ref[1],
        sine * table_ref[0] + cosine * table_ref[1],
    )


def turned(tile, cosine, sine, sign):
    rows = tile.shape[0]
    first = (lax.broadcasted_iota(jnp.int32, (rows, 128), 1) % HEAD_DIM) < HEAD_DIM // 2
    partner = jnp.where(first, -sign * pltpu.roll(tile, 96, 1), sign * pltpu.roll(tile, 32, 1))
    return tile * cosine + partner * sine


def start_of(position, bounds_ref):
    begin = jnp.zeros_like(position)
    for i in range(3):
        bound = bounds_ref[i]
        begin = jnp.where(position >= bound, bound, begin)
    return begin


def scalar_start(position, bounds_ref):
    begin = jnp.int32(0)
    for i in range(3):
        bound = bounds_ref[i]
        begin = jnp.where(position >= bound, bound, begin)
    return begin


def copies_of(pairs, sems):
    made = [pltpu.make_async_copy(src, dst, sems.at[i]) for i, (src, dst) in enumerate(pairs)]
    for item in made:
        item.start()
    return made


def pre_kernel(
    me_ref, x_ref, gains_ref, seg_ref, base_ref, table_ref, we_ref, ws_ref, wq_ref, wk_ref, wv_ref,
    *rest,
):
    x1_ref, act_ref = rest[:2]
    packets = rest[2:10]
    we, ws, wqkv, stage, sems = rest[10:]
    chunks = we.shape[0]
    wide = we.shape[2]
    pairs = []
    for c in range(chunks):
        pairs.append((we_ref.at[:, pl.ds(c * wide, wide)], we.at[c]))
        pairs.append((ws_ref.at[pl.ds(c * wide, wide), :], ws.at[c]))
    for i, ref in enumerate((wq_ref, wk_ref, wv_ref)):
        pairs.append((ref, wqkv.at[i]))
    copies = copies_of(pairs, sems)
    me = me_ref[0]
    own = me % HEADS
    gains = gains_ref[...].astype(F32)
    x = x_ref[...].astype(F32)
    normed, _ = norm(x)
    hidden = (normed * gains[0:1]).astype(BF16)
    total = jnp.zeros(x.shape, F32)
    for c in range(chunks):
        copies[2 * c].wait()
        act = mm(hidden, we[c])
        act_ref[:, c * wide : (c + 1) * wide] = act.astype(BF16)
        copies[2 * c + 1].wait()
        total = total + mm((act * jax.nn.sigmoid(act)).astype(BF16), ws[c])
    x1 = x + 0.5 * total
    x1_ref[...] = x1
    normed, _ = norm(x1)
    hidden = (normed * gains[1:2]).astype(BF16)
    cosine, sine = angles(base_ref, table_ref, me)
    rows = x.shape[0]
    half = rows // 2
    low = low_lanes(rows)
    low_half = low_lanes(half)
    for i in range(3):
        copies[2 * chunks + i].wait()
    query = mm(hidden, wqkv[0])
    key = mm(hidden, wqkv[1])
    value = mm(hidden, wqkv[2])
    for p in range(HEADS // 2):
        lanes = slice(128 * p, 128 * p + 128)
        q = turned(query[:, lanes], cosine, sine, 1.0) * 0.125
        k = turned(key[:, lanes], cosine, sine, 1.0)
        v = value[:, lanes]
        even = jnp.where(low, q, pltpu.roll(k, HEAD_DIM, 1))
        odd = jnp.where(low, pltpu.roll(q, HEAD_DIM, 1), k)
        v_even = jnp.where(low_half, v[:half], pltpu.roll(v[half:], HEAD_DIM, 1))
        v_odd = jnp.where(low_half, pltpu.roll(v[:half], HEAD_DIM, 1), v[half:])
        for head, qk, vv in ((2 * p, even, v_even), (2 * p + 1, odd, v_odd)):
            stage[head, :rows] = qk.astype(BF16)
            stage[head, rows : rows + half] = vv.astype(BF16)
    for i in range(HEADS):
        packets[i][: rows + half, :] = stage[own ^ i]
        packets[i][rows + half :, :] = seg_ref[...]


def call_pre(me, x, gains, seg, base, table, we, ws, wq, wk, wv):
    rows, width = x.shape
    hidden = we.shape[1]
    wide = 512
    chunks = hidden // wide
    packet = rows + rows // 2 + 16
    return pl.pallas_call(
        pre_kernel,
        name="pre",
        out_shape=(
            jax.ShapeDtypeStruct((rows, width), F32),
            jax.ShapeDtypeStruct((rows, hidden), BF16),
        )
        + (jax.ShapeDtypeStruct((packet, 128), BF16),) * HEADS,
        in_specs=[SMEM] + [VMEM] * 5 + [ANY] * 5,
        out_specs=(VMEM,) * (2 + HEADS),
        scratch_shapes=[
            pltpu.VMEM((chunks, width, wide), BF16),
            pltpu.VMEM((chunks, wide, width), BF16),
            pltpu.VMEM((3, width, width), BF16),
            pltpu.VMEM((HEADS, rows + rows // 2, 128), BF16),
            pltpu.SemaphoreType.DMA((2 * chunks + 3,)),
        ],
    )(me, x, gains, seg, base, table, we, ws, wq, wk, wv)


def unpack_kernel(groups, me_ref, bounds_in, *rest):
    packets = rest[:HEADS]
    q_ref, k_ref, v_ref, bounds_ref = rest[HEADS:]
    unpack(groups, me_ref, bounds_in, packets, q_ref, k_ref, v_ref, bounds_ref)


def unpack(groups, me_ref, bounds_in, packets, q_ref, k_ref, v_ref, bounds_ref):
    rows = TILE
    half = rows // 2
    own = me_ref[0] % HEADS
    counts = [jnp.zeros((16, 128), F32) for _ in range(3)]
    for i in range(HEADS):
        source = own ^ i
        at = pl.multiple_of(source * rows, rows)
        q_ref[pl.ds(at, rows), :] = packets[i][:rows, :HEAD_DIM]
        k_ref[pl.ds(at, rows), :] = packets[i][:rows, HEAD_DIM:]
        v_ref[pl.ds(at, half), :] = packets[i][rows : rows + half, :HEAD_DIM]
        v_ref[pl.ds(at + half, half), :] = packets[i][rows : rows + half, HEAD_DIM:]
        if groups == 1:
            ids = packets[i][rows + half :, :].astype(F32)
            for s in range(3):
                counts[s] = counts[s] + jnp.where(ids < s + 1.0, 1.0, 0.0)
    for s in range(3):
        if groups == 1:
            bounds_ref[s] = jnp.sum(counts[s]).astype(jnp.int32)
        else:
            bounds_ref[s] = bounds_in[s]


def forward_blocks(first, bounds_ref, q_ref, k_ref, v_ref, vt, scores, ot_ref, lse_ref, rows_ref):
    blocks = q_ref.shape[0] // TILE

    def transpose_value(kb, carry):
        at = pl.multiple_of(kb * TILE, TILE)
        vt[kb] = v_ref[pl.ds(at, TILE), :].T
        return carry

    lax.fori_loop(0, v_ref.shape[0] // TILE, transpose_value, 0)

    def block(qb, carry):
        at = pl.multiple_of(qb * TILE, TILE)
        begin = first + qb * TILE
        query = q_ref[pl.ds(at, TILE), :]
        position = begin + lax.broadcasted_iota(jnp.int32, (1, TILE), 1)
        starts = start_of(position, bounds_ref)
        lowest = scalar_start(begin, bounds_ref) // TILE
        highest = begin // TILE + 1

        def score(kb, top):
            key = k_ref[pl.ds(pl.multiple_of(kb * TILE, TILE), TILE), :]
            where_key = kb * TILE + lax.broadcasted_iota(jnp.int32, (TILE, TILE), 0)
            seen = (where_key <= position) & (where_key >= starts)
            tile = jnp.where(seen, mm_nt(key, query), -1e30)
            scores[kb - lowest] = tile
            return jnp.maximum(top, jnp.max(tile, axis=0, keepdims=True))

        top = lax.fori_loop(lowest, highest, score, jnp.full((1, TILE), -1e30, F32))

        def weigh(kb, state):
            sums, out = state
            weights = jnp.exp(scores[kb - lowest] - top)
            return (
                sums + jnp.sum(weights, axis=0, keepdims=True),
                out + mm(vt[kb], weights.astype(BF16)),
            )

        sums, out = lax.fori_loop(
            lowest,
            highest,
            weigh,
            (jnp.zeros((1, TILE), F32), jnp.zeros((HEAD_DIM, TILE), F32)),
        )
        out = out / sums
        ot_ref[qb] = out
        lse_ref[qb] = top + jnp.log(sums)
        padded = jnp.concatenate([out, jnp.zeros((128 - HEAD_DIM, TILE), F32)], axis=0)
        rows_ref[pl.ds(at + EDGE, TILE), :] = padded.T
        return carry

    lax.fori_loop(0, blocks, block, 0)


def forward_kernel(groups, me_ref, bounds_in, *rest):
    if groups == 1:
        packets = rest[:HEADS]
        rest = rest[HEADS:]
    else:
        q_ref, k_ref, v_ref = rest[:3]
        rest = rest[3:]
    outs = rest[:HEADS]
    ot_ref, lse_ref = rest[HEADS : HEADS + 2]
    rest = rest[HEADS + 2 :]
    if groups == 1:
        q_ref, k_ref, v_ref, bounds_ref = rest[:4]
        rest = rest[4:]
        unpack(groups, me_ref, bounds_in, packets, q_ref, k_ref, v_ref, bounds_ref)
    else:
        bounds_ref = bounds_in
    vt, scores, rows_ref = rest
    me = me_ref[0]
    own = me % HEADS
    length = q_ref.shape[0]
    rows_ref[:EDGE, :] = jnp.zeros((EDGE, 128), F32)
    rows_ref[EDGE + length :, :] = jnp.zeros((EDGE, 128), F32)
    forward_blocks(
        (me // HEADS) * length, bounds_ref, q_ref, k_ref, v_ref, vt, scores, ot_ref, lse_ref,
        rows_ref,
    )
    half = TILE // 2
    for i in range(HEADS):
        at = pl.multiple_of((own ^ i) * TILE, TILE)
        outs[i][:half, :] = joined(
            rows_ref[pl.ds(at + EDGE, half), :], rows_ref[pl.ds(at + EDGE + half, half), :], half
        ).astype(BF16)
        outs[i][half:, :] = joined(
            rows_ref[pl.ds(at, EDGE), :], rows_ref[pl.ds(at + EDGE + TILE, EDGE), :], EDGE
        ).astype(BF16)


def call_forward(groups, me, bounds, operands, length):
    blocks = length // TILE
    total = blocks * groups
    saved = ()
    saved_specs = ()
    if groups == 1:
        saved = (jax.ShapeDtypeStruct((length, HEAD_DIM), BF16),) * 3 + (
            jax.ShapeDtypeStruct((8,), jnp.int32),
        )
        saved_specs = (VMEM,) * 3 + (SMEM,)
    return pl.pallas_call(
        functools.partial(forward_kernel, groups),
        name="attend",
        out_shape=(jax.ShapeDtypeStruct((TILE // 2 + EDGE, 128), BF16),) * HEADS
        + (
            jax.ShapeDtypeStruct((blocks, HEAD_DIM, TILE), F32),
            jax.ShapeDtypeStruct((blocks, 1, TILE), F32),
        )
        + saved,
        in_specs=[SMEM, SMEM] + [VMEM] * len(operands),
        out_specs=(VMEM,) * (HEADS + 2) + saved_specs,
        scratch_shapes=[
            pltpu.VMEM((total, HEAD_DIM, TILE), BF16),
            pltpu.VMEM((total, TILE, TILE), F32),
            pltpu.VMEM((length + 2 * EDGE, 128), F32),
        ],
    )(me, bounds, *operands)


def call_unpack(groups, me, bounds, packets, length):
    return pl.pallas_call(
        functools.partial(unpack_kernel, groups),
        name="unpack",
        out_shape=(jax.ShapeDtypeStruct((length, HEAD_DIM), BF16),) * 3
        + (jax.ShapeDtypeStruct((8,), jnp.int32),),
        in_specs=[SMEM, SMEM] + [VMEM] * HEADS,
        out_specs=(VMEM,) * 3 + (SMEM,),
    )(me, bounds, *packets)


def backward_kernel(groups, me_ref, bounds_ref, q_ref, k_ref, v_ref, ot_ref, lse_ref, *rest):
    grads = rest[:HEADS]
    rest = rest[HEADS:]
    if groups == 1:
        base_ref, table_ref = rest[:2]
        outs = rest[2 : 2 + HEADS]
        rest = rest[2 + HEADS :]
        dq_ref, dk_ref, dv_ref = rest[:3]
        rest = rest[3:]
    else:
        dq_ref, dk_ref, dv_ref = rest[:3]
        rest = rest[3:]
    kt, do_ref, delta_ref = rest
    me = me_ref[0]
    own = me % HEADS
    length = q_ref.shape[0]
    blocks = length // TILE
    first = (me // HEADS) * length
    half = TILE // 2
    for i in range(HEADS):
        source = own ^ i
        at = pl.multiple_of(source * TILE, TILE)
        do_ref[pl.ds(at, half), :] = grads[i][:, :HEAD_DIM]
        do_ref[pl.ds(at + half, half), :] = grads[i][:, HEAD_DIM:]

    def prepare_key(kb, carry):
        at = pl.multiple_of(kb * TILE, TILE)
        kt[kb] = k_ref[pl.ds(at, TILE), :].T
        dk_ref[pl.ds(at, TILE), :] = jnp.zeros((TILE, HEAD_DIM), F32)
        dv_ref[pl.ds(at, TILE), :] = jnp.zeros((TILE, HEAD_DIM), F32)
        return carry

    lax.fori_loop(0, k_ref.shape[0] // TILE, prepare_key, 0)

    def prepare_query(qb, carry):
        at = pl.multiple_of(qb * TILE, TILE)
        gradient = do_ref[pl.ds(at, TILE), :].T.astype(F32)
        delta_ref[qb] = jnp.sum(gradient * ot_ref[qb], axis=0, keepdims=True)
        return carry

    lax.fori_loop(0, blocks, prepare_query, 0)

    def block(qb, carry):
        at = pl.multiple_of(qb * TILE, TILE)
        begin = first + qb * TILE
        query = q_ref[pl.ds(at, TILE), :]
        gradient = do_ref[pl.ds(at, TILE), :]
        lse = lse_ref[qb]
        delta = delta_ref[qb]
        position = begin + lax.broadcasted_iota(jnp.int32, (1, TILE), 1)
        starts = start_of(position, bounds_ref)
        lowest = scalar_start(begin, bounds_ref) // TILE
        highest = begin // TILE + 1

        def step(kb, dqt):
            here = pl.ds(pl.multiple_of(kb * TILE, TILE), TILE)
            key = k_ref[here, :]
            where_key = kb * TILE + lax.broadcasted_iota(jnp.int32, (TILE, TILE), 0)
            seen = (where_key <= position) & (where_key >= starts)
            weights = jnp.exp(jnp.where(seen, mm_nt(key, query) - lse, -1e30))
            ds = (weights * (mm_nt(v_ref[here, :], gradient) - delta)).astype(BF16)
            dv_ref[here, :] += mm(weights.astype(BF16), gradient)
            dk_ref[here, :] += mm(ds, query)
            return dqt + mm(kt[kb], ds)

        dqt = lax.fori_loop(lowest, highest, step, jnp.zeros((HEAD_DIM, TILE), F32))
        padded = jnp.concatenate([dqt, jnp.zeros((128 - HEAD_DIM, TILE), F32)], axis=0)
        dq_ref[pl.ds(at, TILE), :] = padded.T[:, :HEAD_DIM]
        return carry

    lax.fori_loop(0, blocks, block, 0)
    if groups == 1:
        pack(me, base_ref, table_ref, dq_ref, dk_ref, dv_ref, outs)


def pack(me, base_ref, table_ref, dq_ref, dk_ref, dv_ref, outs):
    own = me % HEADS
    half = TILE // 2
    scale = jnp.where(low_lanes(TILE), 0.125, 1.0)
    for i in range(HEADS):
        source = own ^ i
        at = pl.multiple_of(source * TILE, TILE)
        cosine, sine = angles(base_ref, table_ref, me ^ i)
        tile = jnp.concatenate([dq_ref[pl.ds(at, TILE), :], dk_ref[pl.ds(at, TILE), :]], axis=1)
        outs[i][:TILE, :] = (turned(tile, cosine, sine, -1.0) * scale).astype(BF16)
        outs[i][TILE:, :] = jnp.concatenate(
            [dv_ref[pl.ds(at, half), :], dv_ref[pl.ds(at + half, half), :]], axis=1
        ).astype(BF16)


def pack_kernel(me_ref, base_ref, table_ref, dq_ref, dk_ref, dv_ref, *outs):
    pack(me_ref[0], base_ref, table_ref, dq_ref, dk_ref, dv_ref, outs)


def call_backward(groups, me, bounds, saved, ot, lse, grads, base, table):
    length = saved[0].shape[0]
    blocks = length // TILE
    total = blocks * groups
    packets = (jax.ShapeDtypeStruct((TILE + TILE // 2, 128), BF16),) * HEADS
    scratch = [
        pltpu.VMEM((total, HEAD_DIM, TILE), BF16),
        pltpu.VMEM((length, HEAD_DIM), BF16),
        pltpu.VMEM((blocks, 1, TILE), F32),
    ]
    if groups == 1:
        return pl.pallas_call(
            functools.partial(backward_kernel, groups),
            name="attend_back",
            out_shape=packets,
            in_specs=[SMEM, SMEM] + [VMEM] * (7 + HEADS),
            out_specs=(VMEM,) * HEADS,
            scratch_shapes=[pltpu.VMEM((length, HEAD_DIM), F32)] * 3 + scratch,
        )(me, bounds, *saved, ot, lse, *grads, base, table)
    dq, dk, dv = pl.pallas_call(
        functools.partial(backward_kernel, groups),
        name="attend_back",
        out_shape=(
            jax.ShapeDtypeStruct((length, HEAD_DIM), F32),
            jax.ShapeDtypeStruct((length * groups, HEAD_DIM), F32),
            jax.ShapeDtypeStruct((length * groups, HEAD_DIM), F32),
        ),
        in_specs=[SMEM, SMEM] + [VMEM] * (5 + HEADS),
        out_specs=(VMEM,) * 3,
        scratch_shapes=scratch,
    )(me, bounds, *saved, ot, lse, *grads)
    across = [[g * HEADS + a for g in range(groups)] for a in range(HEADS)]
    both = lax.psum_scatter(
        jnp.concatenate([dk, dv], axis=1), "tm", scatter_dimension=0, axis_index_groups=across,
        tiled=True,
    )
    return pl.pallas_call(
        pack_kernel,
        name="pack",
        out_shape=packets,
        in_specs=[SMEM] + [VMEM] * 5,
        out_specs=(VMEM,) * HEADS,
    )(me, base, table, dq, both[:, :HEAD_DIM], both[:, HEAD_DIM:])


def mid_kernel(
    total, me_ref, bounds_ref, *rest,
):
    packets = rest[:HEADS]
    rest = rest[HEADS:]
    (
        x1_ref, before_ref, after_ref, cot_ref, cot_after_ref, gains_ref, depth_ref,
        wo_ref, wce_ref, wcs_ref, we_ref, ws_ref,
    ) = rest[:12]
    rest = rest[12:]
    out_ref, dx2_ref, small_ref = rest[:3]
    att_ref, da_low_ref, h3_ref, dc_ref, z_ref, dz_ref, h4_ref, dact_ref, s_ref, df_ref = rest[3:13]
    outs = rest[13 : 13 + HEADS]
    (
        wo, wce, wcs, we, ws, stage, att, x2, u_all, act, dm_all, gs, sems,
    ) = rest[13 + HEADS :]
    chunks = we.shape[0]
    wide = we.shape[2]
    pairs = [(wo_ref, wo), (wce_ref, wce), (wcs_ref, wcs)]
    for c in range(chunks):
        pairs.append((we_ref.at[:, pl.ds(c * wide, wide)], we.at[c]))
        pairs.append((ws_ref.at[pl.ds(c * wide, wide), :], ws.at[c]))
    copies = copies_of(pairs, sems)
    me = me_ref[0]
    own = me % HEADS
    rows = x1_ref.shape[0]
    width = x1_ref.shape[1]
    half = rows // 2
    long = rows + 2 * EDGE
    tail = rows + EDGE
    gains = gains_ref[...].astype(F32)
    depth = depth_ref[...].astype(F32)
    taps = depth.shape[0]
    for i in range(HEADS):
        stage[own ^ i] = packets[i][...].astype(F32)
    for p in range(HEADS // 2):
        lanes = slice(128 * p, 128 * p + 128)
        even, odd = stage[2 * p], stage[2 * p + 1]
        for top, rest_rows, dest in (
            (0, half, EDGE),
            (half, EDGE, None),
        ):
            e, o = even[top : top + rest_rows], odd[top : top + rest_rows]
            low = low_lanes(rest_rows)
            left = jnp.where(low, e, pltpu.roll(o, HEAD_DIM, 1)).astype(BF16)
            right = jnp.where(low, pltpu.roll(e, HEAD_DIM, 1), o).astype(BF16)
            if dest is None:
                att[:EDGE, lanes] = left
                att[EDGE + rows :, lanes] = right
            else:
                att[EDGE : EDGE + half, lanes] = left
                att[EDGE + half : EDGE + rows, lanes] = right
    att_ref[...] = att[EDGE : EDGE + rows, :]
    copies[0].wait()
    product = mm(att[...], wo[...])
    x2[:EDGE] = before_ref[...] + product[:EDGE]
    x2[EDGE : EDGE + rows] = x1_ref[...] + product[EDGE : EDGE + rows]
    x2[EDGE + rows :] = after_ref[...] + product[EDGE + rows :]
    n3, inv3 = norm(x2[...])
    h3 = (n3 * gains[2:3]).astype(BF16)
    h3_ref[...] = h3[EDGE : EDGE + rows]
    copies[1].wait()
    linear = mm(h3, wce[:, :width])
    gate = jax.nn.sigmoid(mm(h3, wce[:, width:]))
    u_all[...] = (linear * gate).astype(BF16).astype(F32)
    linear = linear[EDGE : EDGE + rows]
    gate = gate[EDGE : EDGE + rows]
    frame = me * rows + lax.broadcasted_iota(jnp.int32, (tail, 128), 0)
    since = frame - start_of(frame, bounds_ref)
    since = jnp.where(frame < total, since, -1)
    mixed = jnp.zeros((tail, width), F32)
    u_long = u_all[...]
    for j in range(taps):
        moved = u_long[EDGE - j : EDGE - j + tail]
        keep = jnp.tile(since >= j, (1, width // 128))
        mixed = mixed + jnp.where(keep, depth[j : j + 1] * moved, 0.0)
    nm, invm = norm(mixed)
    inner = nm * gains[3:4]
    z = (inner * jax.nn.sigmoid(inner)).astype(BF16)
    z_ref[...] = z[:rows]
    copies[2].wait()
    x3 = x2[EDGE:] + mm(z, wcs[...])
    n4, inv4 = norm(x3)
    h4 = (n4 * gains[4:5]).astype(BF16)
    h4_ref[...] = h4[:rows]
    grown = jnp.zeros((tail, width), F32)
    for c in range(chunks):
        copies[3 + 2 * c].wait()
        a = mm(h4, we[c])
        act[c] = a
        s = (a * jax.nn.sigmoid(a)).astype(BF16)
        s_ref[:, c * wide : (c + 1) * wide] = s[:rows]
        copies[4 + 2 * c].wait()
        grown = grown + mm(s, ws[c])
    x4 = x3 + 0.5 * grown
    n5, inv5 = norm(x4)
    out_ref[...] = (n5[:rows] * gains[5:6]).astype(BF16)
    cot = jnp.concatenate([cot_ref[...].astype(F32), cot_after_ref[...].astype(F32)], axis=0)
    small_ref[...] = jnp.zeros(small_ref.shape, F32)
    small_ref[5:6] = jnp.sum(cot[:rows] * n5[:rows], axis=0, keepdims=True)
    dx4 = norm_back(cot * gains[5:6], n5, inv5)
    df = (0.5 * dx4).astype(BF16)
    df_ref[...] = df[:rows]
    dh = jnp.zeros((tail, width), F32)
    for c in range(chunks):
        da = (mm_nt(df, ws[c]) * swish_grad(act[c])).astype(BF16)
        dact_ref[:, c * wide : (c + 1) * wide] = da[:rows]
        dh = dh + mm_nt(da, we[c])
    small_ref[4:5] = jnp.sum(dh[:rows] * n4[:rows], axis=0, keepdims=True)
    dx3 = dx4 + norm_back(dh * gains[4:5], n4, inv4)
    dz = dx3.astype(BF16)
    dz_ref[...] = dz[:rows]
    dg = mm_nt(dz, wcs[...]) * swish_grad(inner)
    small_ref[3:4] = jnp.sum(dg[:rows] * nm[:rows], axis=0, keepdims=True)
    dm = norm_back(dg * gains[3:4], nm, invm)
    du = jnp.zeros((rows, width), F32)
    u_own = u_all[EDGE : EDGE + rows]
    for j in range(taps):
        keep = jnp.tile(since >= j, (1, width // 128))
        moved = jnp.where(keep, dm, 0.0)[j : j + rows]
        small_ref[8 + j : 9 + j] = jnp.sum(moved * u_own, axis=0, keepdims=True)
        du = du + depth[j : j + 1] * moved
    dc_one = (du * gate).astype(BF16)
    dc_two = (du * linear * gate * (1.0 - gate)).astype(BF16)
    dc_ref[:, :width] = dc_one
    dc_ref[:, width:] = dc_two
    dh = mm_nt(dc_one, wce[:, :width]) + mm_nt(dc_two, wce[:, width:])
    n3 = n3[EDGE : EDGE + rows]
    small_ref[2:3] = jnp.sum(dh * n3, axis=0, keepdims=True)
    dx2 = dx3[:rows] + norm_back(dh * gains[2:3], n3, inv3[EDGE : EDGE + rows])
    dx2_ref[...] = dx2
    low_grad = dx2.astype(BF16)
    da_low_ref[...] = low_grad
    do = mm_nt(low_grad, wo[...])
    low = low_lanes(half)
    for p in range(HEADS // 2):
        lanes = slice(128 * p, 128 * p + 128)
        top, bottom = do[:half, lanes], do[half:, lanes]
        gs[2 * p] = jnp.where(low, top, pltpu.roll(bottom, HEAD_DIM, 1)).astype(BF16)
        gs[2 * p + 1] = jnp.where(low, pltpu.roll(top, HEAD_DIM, 1), bottom).astype(BF16)
    for i in range(HEADS):
        outs[i][...] = gs[own ^ i]


def call_mid(total, me, bounds, packets, *operands):
    x1 = operands[0]
    wo, wce, wcs, we, ws = operands[7:]
    rows, width = x1.shape
    hidden = we.shape[1]
    wide = 512
    chunks = hidden // wide
    long = rows + 2 * EDGE
    tail = rows + EDGE

    def low(*shape):
        return jax.ShapeDtypeStruct(shape, BF16)

    return pl.pallas_call(
        functools.partial(mid_kernel, total),
        name="middle",
        out_shape=(
            low(rows, width),
            jax.ShapeDtypeStruct((rows, width), F32),
            jax.ShapeDtypeStruct((24, width), F32),
            low(rows, width),
            low(rows, width),
            low(rows, width),
            low(rows, 2 * width),
            low(rows, width),
            low(rows, width),
            low(rows, width),
            low(rows, hidden),
            low(rows, hidden),
            low(rows, width),
        )
        + (low(rows // 2, 128),) * HEADS,
        in_specs=[SMEM, SMEM] + [VMEM] * (HEADS + 7) + [ANY] * 5,
        out_specs=(VMEM,) * (13 + HEADS),
        scratch_shapes=[
            pltpu.VMEM((width, width), BF16),
            pltpu.VMEM((width, 2 * width), BF16),
            pltpu.VMEM((width, width), BF16),
            pltpu.VMEM((chunks, width, wide), BF16),
            pltpu.VMEM((chunks, wide, width), BF16),
            pltpu.VMEM((HEADS, rows // 2 + EDGE, 128), F32),
            pltpu.VMEM((long, width), BF16),
            pltpu.VMEM((long, width), F32),
            pltpu.VMEM((long, width), F32),
            pltpu.VMEM((chunks, tail, wide), F32),
            pltpu.VMEM((tail, width), F32),
            pltpu.VMEM((HEADS, rows // 2, 128), BF16),
            pltpu.SemaphoreType.DMA((3 + 2 * chunks,)),
        ],
    )(me, bounds, *packets, *operands)


def post_kernel(me_ref, *rest):
    packets = rest[:HEADS]
    rest = rest[HEADS:]
    (
        x_ref, x1_ref, dx2_ref, act_ref, gains_ref, wq_ref, wk_ref, wv_ref, we_ref, ws_ref,
    ) = rest[:10]
    rest = rest[10:]
    grad_ref, small_ref, h2_ref, dq_ref, dk_ref, dv_ref, h1_ref, da_ref, s_ref, df_ref = rest[:10]
    we, ws, wqkv, stage, sems = rest[10:]
    chunks = we.shape[0]
    wide = we.shape[2]
    pairs = [(ref, wqkv.at[i]) for i, ref in enumerate((wq_ref, wk_ref, wv_ref))]
    for c in range(chunks):
        pairs.append((ws_ref.at[pl.ds(c * wide, wide), :], ws.at[c]))
        pairs.append((we_ref.at[:, pl.ds(c * wide, wide)], we.at[c]))
    copies = copies_of(pairs, sems)
    own = me_ref[0] % HEADS
    rows, width = x_ref.shape
    half = rows // 2
    gains = gains_ref[...].astype(F32)
    low = low_lanes(rows)
    low_half = low_lanes(half)
    for i in range(HEADS):
        stage[own ^ i] = packets[i][...].astype(F32)
    for p in range(HEADS // 2):
        lanes = slice(128 * p, 128 * p + 128)
        even, odd = stage[2 * p], stage[2 * p + 1]
        e, o = even[:rows], odd[:rows]
        dq_ref[:, lanes] = jnp.where(low, e, pltpu.roll(o, HEAD_DIM, 1)).astype(BF16)
        dk_ref[:, lanes] = jnp.where(low, pltpu.roll(e, HEAD_DIM, 1), o).astype(BF16)
        e, o = even[rows:], odd[rows:]
        dv_ref[:half, lanes] = jnp.where(low_half, e, pltpu.roll(o, HEAD_DIM, 1)).astype(BF16)
        dv_ref[half:, lanes] = jnp.where(low_half, pltpu.roll(e, HEAD_DIM, 1), o).astype(BF16)
    x1 = x1_ref[...]
    n2, inv2 = norm(x1)
    h2_ref[...] = (n2 * gains[1:2]).astype(BF16)
    for i in range(3):
        copies[i].wait()
    dh = (
        mm_nt(dq_ref[...], wqkv[0]) + mm_nt(dk_ref[...], wqkv[1]) + mm_nt(dv_ref[...], wqkv[2])
    )
    small_ref[...] = jnp.zeros(small_ref.shape, F32)
    small_ref[1:2] = jnp.sum(dh * n2, axis=0, keepdims=True)
    dx1 = dx2_ref[...] + norm_back(dh * gains[1:2], n2, inv2)
    df = (0.5 * dx1).astype(BF16)
    df_ref[...] = df
    x = x_ref[...].astype(F32)
    n1, inv1 = norm(x)
    h1_ref[...] = (n1 * gains[0:1]).astype(BF16)
    dh = jnp.zeros((rows, width), F32)
    for c in range(chunks):
        span = slice(c * wide, (c + 1) * wide)
        act = act_ref[:, span].astype(F32)
        squashed = jax.nn.sigmoid(act)
        s_ref[:, span] = (act * squashed).astype(BF16)
        copies[3 + 2 * c].wait()
        da = (mm_nt(df, ws[c]) * (squashed * (1.0 + act * (1.0 - squashed)))).astype(BF16)
        da_ref[:, span] = da
        copies[4 + 2 * c].wait()
        dh = dh + mm_nt(da, we[c])
    small_ref[0:1] = jnp.sum(dh * n1, axis=0, keepdims=True)
    grad_ref[...] = (dx1 + norm_back(dh * gains[0:1], n1, inv1)).astype(BF16)


def call_post(me, packets, *operands):
    x = operands[0]
    we = operands[8]
    rows, width = x.shape
    hidden = we.shape[1]
    wide = 512
    chunks = hidden // wide

    def low(*shape):
        return jax.ShapeDtypeStruct(shape, BF16)

    return pl.pallas_call(
        post_kernel,
        name="post",
        out_shape=(
            low(rows, width),
            jax.ShapeDtypeStruct((8, width), F32),
            low(rows, width),
            low(rows, width),
            low(rows, width),
            low(rows, width),
            low(rows, width),
            low(rows, hidden),
            low(rows, hidden),
            low(rows, width),
        ),
        in_specs=[SMEM] + [VMEM] * (HEADS + 5) + [ANY] * 5,
        out_specs=(VMEM,) * 10,
        scratch_shapes=[
            pltpu.VMEM((chunks, width, wide), BF16),
            pltpu.VMEM((chunks, wide, width), BF16),
            pltpu.VMEM((3, width, width), BF16),
            pltpu.VMEM((HEADS, rows + rows // 2, 128), F32),
            pltpu.SemaphoreType.DMA((3 + 2 * chunks,)),
        ],
    )(me, *packets, *operands)


def layout_rows(jobs, count):
    table = []
    at = 0
    for left, right in jobs:
        shard = left // count
        table.append((at, shard, right // 512))
        at += shard * (right // 512)
    return table, at


def weight_kernel(jobs, me_ref, *rest):
    count = len(jobs)
    operands = rest[: 2 * count]
    kept_ref, sent_ref = rest[2 * count : 2 * count + 2]
    scratch = rest[2 * count + 2 :]
    own = me_ref[0] % HEADS
    table, _ = layout_rows(jobs, HEADS)
    for job, (at, shard, parts) in enumerate(table):
        left, right = operands[2 * job], operands[2 * job + 1]
        turned_ref, ordered_ref = scratch[2 * job : 2 * job + 2]
        tall = left.shape[1]
        for c in range(tall // 512):
            turned_ref[c * 512 : (c + 1) * 512] = left[:, c * 512 : (c + 1) * 512].T
        for place, i in enumerate(ORDER):
            ordered_ref[place * shard : (place + 1) * shard] = turned_ref[
                pl.ds(pl.multiple_of((own ^ i) * shard, shard), shard), :
            ]
        for c in range(parts):
            factor = right[:, c * 512 : (c + 1) * 512]
            for block in range(tall // 512):
                span = 512
                product = mm(ordered_ref[block * span : (block + 1) * span], factor).astype(BF16)
                for piece in range(span // shard):
                    place = block * (span // shard) + piece
                    dest = kept_ref if place < 4 else sent_ref
                    dest[place % 4, at + c * shard : at + (c + 1) * shard] = product[
                        piece * shard : (piece + 1) * shard
                    ]


def call_weights(jobs, me, operands, name):
    _, rows = layout_rows(jobs, HEADS)
    frames = operands[0].shape[0]
    return pl.pallas_call(
        functools.partial(weight_kernel, jobs),
        name=name,
        out_shape=(jax.ShapeDtypeStruct((4, rows, 512), BF16),) * 2,
        in_specs=[SMEM] + [VMEM] * len(operands),
        out_specs=(VMEM,) * 2,
        scratch_shapes=[
            pltpu.VMEM((left, frames), BF16) for left, _ in jobs for _ in range(2)
        ],
    )(me, *operands)


def finish_kernel(jobs, count, row_ref, *rest):
    pieces = rest[:4]
    outs = rest[4 : 4 + len(jobs)]
    (held,) = rest[4 + len(jobs) :]
    row = row_ref[0]
    size = pieces[0].shape[0]
    for j in range(4):
        held[pl.ds(pl.multiple_of((row ^ j) * size, size), size), :] = pieces[j][...]
    table, _ = layout_rows(jobs, count)
    for (at, shard, parts), out in zip(table, outs):
        for c in range(parts):
            out[:, c * 512 : (c + 1) * 512] = held[
                at + c * shard : at + (c + 1) * shard, :
            ].astype(F32)


def call_finish(jobs, count, row, pieces, name):
    table, rows = layout_rows(jobs, count)
    return pl.pallas_call(
        functools.partial(finish_kernel, jobs, count),
        name=name,
        out_shape=tuple(
            jax.ShapeDtypeStruct((left // count, right), F32) for left, right in jobs
        ),
        in_specs=[SMEM] + [VMEM] * 4,
        out_specs=(VMEM,) * len(jobs),
        scratch_shapes=[pltpu.VMEM((rows, 512), BF16)],
    )(row, *pieces)


def weight_sums(jobs, me, row, operands, name):
    count = lax.axis_size("tm")
    if count == HEADS:
        kept, sent = call_weights(jobs, me, operands, name)
        return call_finish(jobs, count, row, sum_relative(kept, sent), name + "_out")
    stacked = []
    for i, (left, right) in enumerate(jobs):
        product = jnp.einsum(
            "fa,fb->ab", operands[2 * i], operands[2 * i + 1], preferred_element_type=F32
        ).astype(BF16)
        shards = product.reshape(count, left // count, right // 512, 512)
        stacked.append(shards.transpose(0, 2, 1, 3).reshape(count, -1, 512))
    pieces = sum_general(jnp.concatenate(stacked, axis=1))
    index = lax.axis_index("rows")
    whole = jnp.concatenate([pieces[0][None]] + [p[None] for p in pieces[1:]], axis=0)
    whole = jnp.take(whole, jnp.arange(4) ^ index, axis=0).reshape(-1, 512).astype(F32)
    table, _ = layout_rows(jobs, count)
    results = []
    for (at, shard, parts), (left, right) in zip(table, jobs):
        item = whole[at : at + shard * parts].reshape(parts, shard, 512)
        results.append(item.transpose(1, 0, 2).reshape(shard, right))
    return results


def shards(
    frames_in,
    segment_ids,
    cotangent,
    gains,
    expand_one,
    shrink_one,
    query_proj,
    key_proj,
    value_proj,
    output_proj,
    conv_expand,
    conv_depth,
    conv_shrink,
    expand_two,
    shrink_two,
):
    rows = frames_in.shape[1]
    width = frames_in.shape[2]
    hidden = expand_one.shape[1]
    count = lax.axis_size("tm")
    groups = count // HEADS
    length = rows * HEADS
    total = rows * count
    index = lax.axis_index("tm")
    me = jnp.full((1,), index, jnp.int32)
    row = jnp.full((1,), lax.axis_index("rows"), jnp.int32)
    frequency = 10000.0 ** (-np.arange(HEAD_DIM // 2) / (HEAD_DIM // 2))
    lane_frequency = np.tile(frequency, 4)
    inner = np.arange(rows)[:, None] * lane_frequency[None]
    outer = np.arange(count)[:, None] * rows * lane_frequency[None]
    table = jnp.asarray(np.stack([np.cos(inner), np.sin(inner)]), F32)
    base = jnp.asarray(np.stack([np.cos(outer), np.sin(outer)], axis=1), F32)
    seg = jnp.pad(
        segment_ids[0].astype(BF16).reshape(rows // 128, 128),
        ((0, 16 - rows // 128), (0, 0)),
        constant_values=9,
    )
    x = frames_in[0]
    cot = cotangent[0]
    x1, act, *packets = call_pre(
        me, x, gains, seg, base, table, expand_one, shrink_one, query_proj, key_proj, value_proj
    )
    packets = all_swapped(packets)
    before = passed_along(x1[rows - EDGE :], "tm", 1)
    after = passed_along(x1[:EDGE], "tm", -1)
    cot_after = passed_along(cot[:EDGE], "tm", -1)
    bounds = jnp.zeros((8,), jnp.int32)
    if groups > 1:
        ids = lax.all_gather(segment_ids[0], "tm", axis=0, tiled=True)
        bounds = jnp.pad(jnp.sum(ids[None] < jnp.arange(1, 4)[:, None], axis=1), (0, 5)).astype(
            jnp.int32
        )
        *saved, bounds = call_unpack(groups, me, bounds, packets, length)
        across = [[g * HEADS + a for g in range(groups)] for a in range(HEADS)]
        keys, values = (
            lax.all_gather(item, "tm", axis=0, tiled=True, axis_index_groups=across)
            for item in saved[1:]
        )
        saved = (saved[0], keys, values)
        *attended, ot, lse = call_forward(groups, me, bounds, saved, length)
        edge_first = [item[: TILE // 2 + EDGE][:EDGE, :HEAD_DIM] for item in attended]
        edge_last = [item[TILE // 2 - EDGE : TILE // 2, HEAD_DIM:] for item in attended]
        place = index % HEADS
        first_rows = jnp.take(jnp.stack(edge_first), place, axis=0)
        last_rows = jnp.take(jnp.stack(edge_last), place ^ (HEADS - 1), axis=0)
        from_before = passed_along(last_rows, "tm", HEADS)
        from_after = passed_along(first_rows, "tm", -HEADS)
        for i in range(HEADS):
            dest = place ^ i
            edges = attended[i][TILE // 2 :]
            left = jnp.where(dest == 0, from_before, edges[:, :HEAD_DIM])
            right = jnp.where(dest == HEADS - 1, from_after, edges[:, HEAD_DIM:])
            attended[i] = jnp.concatenate(
                [attended[i][: TILE // 2], jnp.concatenate([left, right], axis=1)], axis=0
            )
    else:
        outputs = call_forward(groups, me, bounds, packets, length)
        attended, (ot, lse) = list(outputs[:HEADS]), outputs[HEADS : HEADS + 2]
        *saved, bounds = outputs[HEADS + 2 :]
    attended = all_swapped(attended)
    (
        layer_out, dx2, small_mid, att, da_low, h3, dc, z, dz, h4, dact, s_two, df_two, *grads,
    ) = call_mid(
        total, me, bounds, attended, x1, before, after, cot, cot_after, gains, conv_depth,
        output_proj, conv_expand, conv_shrink, expand_two, shrink_two,
    )
    grads = all_swapped(grads)
    jobs_mid = (
        (width, hidden), (hidden, width), (width, 2 * width), (width, width), (width, width),
    )
    mid_sums = weight_sums(
        jobs_mid, me, row, (h4, dact, s_two, df_two, h3, dc, z, dz, att, da_low), "mid_weights"
    )
    packets = call_backward(groups, me, bounds, saved, ot, lse, grads, base, table)
    packets = all_swapped(packets)
    input_grad, small_post, h2, dq, dk, dv, h1, da, s_one, df_one = call_post(
        me, packets, x, x1, dx2, act, gains, query_proj, key_proj, value_proj, expand_one,
        shrink_one,
    )
    jobs_post = (
        (width, hidden), (hidden, width), (width, width), (width, width), (width, width),
    )
    post_sums = weight_sums(
        jobs_post, me, row, (h1, da, s_one, df_one, h2, dq, h2, dk, h2, dv), "post_weights"
    )
    small = jnp.concatenate([small_post[:2], small_mid[2:6], small_mid[8:23]], axis=0)
    for bit in [1 << i for i in range(count.bit_length() - 1)]:
        small = small + swapped(small, "tm", bit)
    for bit in (1, 2):
        small = small + swapped(small, "rows", bit)
    return (
        layer_out[None],
        input_grad[None],
        small[:6],
        post_sums[0],
        post_sums[1],
        post_sums[2],
        post_sums[3],
        post_sums[4],
        mid_sums[4],
        mid_sums[2],
        small[6:],
        mid_sums[3],
        mid_sums[0],
        mid_sums[1],
    )


def solution(mesh):
    split = P("rows", "tm", None)
    weight = P("tm", None)
    return jax.shard_map(
        shards,
        mesh=mesh,
        in_specs=(split, P("rows", "tm"), split) + (P(),) * 12,
        out_specs=(split, split, P()) + (weight,) * 7 + (P(),) + (weight,) * 3,
        check_vma=False,
    )
```
